128 devices in a mesh: tok: 4 (over y_lo, core), exp: 32 (over x, z, y_hi).
Axes of the slice: x: 4, y: 4 (y_hi: 2, y_lo: 2; y = y_hi * 2 + y_lo), z: 4, core: 2. Of those that a mesh axis runs over, the one named last changes fastest.
Arguments:
- x_tokens: bfloat16 [16384, 4096], P(('tok', 'exp')), may hold values from -48 to 48
- router_weight: bfloat16 [4096, 512], replicated, may hold values from -1 to 1
- gate_rest: float32 [16384, 496], P(('tok', 'exp')), may hold values from -192 to 192
- latent_in: bfloat16 [16384, 1024], P(('tok', 'exp')), may hold values from -6 to 6
- latent_grad: bfloat16 [16384, 1024], P(('tok', 'exp')), may hold values from -6 to 6
- expert_picks: int32 [16384, 22], P('tok'), may hold values from 0 to 511, all different within a row; in each aligned block of 128 rows (0 to 127, 128 to 255, ...) at most 12 rows name the same one
- expert_in: bfloat16 [32, 1024, 1344], P('exp'), may hold values from -0.1875 to 0.1875
- expert_out: bfloat16 [32, 1344, 1024], P('exp'), may hold values from -0.125 to 0.125
Outputs:
- latent_in_grad: bfloat16 [16384, 1024], P(('tok', 'exp'))
- x_grad: bfloat16 [16384, 4096], P(('tok', 'exp'))
- router_weight_grad: float32 [4096, 512], P(('tok', 'exp'))
The draws below stay inside these ranges and needn't reach their ends.
Inputs may be any that keep to these rules, and one draw needn't show every extreme that they name: `expert_picks`: each row names 22 different experts. Within each aligned block of 128 rows (the rows of one device) no expert is named more than 12 times, a bound that some block reaches; every expert is named somewhere.
All inputs are finite; a program needn't handle non-finite values.
Results may differ from the reference program's by a relative error of at most 0.009.
Values may be sent and summed in bfloat16 or wider, within the bound.
No kernel may reach another device: no remote copies, remote signals or barrier semaphores. Data moves between devices by JAX's collectives and lax.ppermute only.
A program may use at most 128 MiB of HBM per device.

```python
import math
import jax
import jax.numpy as jnp
import numpy as np
from jax import lax

D = 4096
L = 1024
H = 2688
EXPERTS = 512
TOP = 22
TOK_DEV = 128
TOKENS = 16384
WIN = 16
HB = 1344
BLOCKS = 32
SLOT_DEPTH = 12


def router_table(key):
    return jax.random.normal(jax.random.fold_in(key, 11), (D, EXPERTS), jnp.float32) * (0.5 / math.sqrt(D))


def draw_router_weight(key, part):
    return router_table(key).astype(jnp.bfloat16)


def draw_x_tokens(key, part):
    base = jnp.clip(jax.random.normal(jax.random.fold_in(key, 12), (TOKENS, D), jnp.float32), -6.0, 6.0)
    result = base
    return result.astype(jnp.bfloat16)


def shard_levels(rng, extent, pieces, least, high):
    gain = 1.0
    for axis_at, shards_of in pieces:
        heights = jax.random.uniform(jax.random.fold_in(jax.random.fold_in(rng, 6), axis_at), (shards_of,), jnp.float32, least / len(pieces), high / len(pieces))
        gain = gain * jnp.repeat(jnp.exp(heights), extent[axis_at] // shards_of).reshape((-1,) + (1,) * (len(extent) - 1 - axis_at))
    return gain


def routed_block(own_key, own, number, rows, number_of, top, most, lean):
    sequence = jax.random.permutation(own_key, number_of)
    heavy_load, ordinary = portions_of(number_of, rows * top, most, lean, True), portions_of(number_of, rows * top, most, lean, False)
    places = jnp.arange(number_of)

    def named(sizes, rotation):
        used = int((sizes > 0).sum())
        fixed = max(1, used // 4)
        shifted = fixed + (places - fixed + rotation * (used - fixed)) % max(1, number_of - fixed)
        return jnp.zeros((number_of,), jnp.int32).at[sequence[jnp.where(places < fixed, places, shifted)]].set(jnp.asarray(sizes, jnp.int32))

    sizes = jnp.where(number % 4 == 0, named(heavy_load, number // 4), named(ordinary, number - number // 4 - 1))
    mixed = jax.random.permutation(jax.random.fold_in(own, 3), number_of)
    source_of, taker = mixed[0:number_of // 2 * 2:2], mixed[1:number_of // 2 * 2:2]
    slack = jnp.minimum(sizes[source_of] - 1, most - sizes[taker]) // 2
    slack = jnp.where((source_of == sequence[0]) | (taker == sequence[0]) | (sizes[taker] == 0), 0, jnp.maximum(slack, 0))
    shifted = jax.random.randint(jax.random.fold_in(own, 4), (number_of // 2,), 0, 1 << 20) % (slack + 1)
    sizes = sizes.at[source_of].add(-shifted).at[taker].add(shifted)
    items = jnp.searchsorted(jnp.cumsum(sizes), jnp.arange(rows * top), side="right").astype(jnp.int32)
    table = items.reshape(top, rows).T
    table = table[jax.random.permutation(jax.random.fold_in(own, 1), rows)]
    rotation = jax.random.randint(jax.random.fold_in(own, 2), (rows, 1), 0, top)
    return jnp.take_along_axis(table, (jnp.arange(top)[None, :] + rotation) % top, axis=1)


def portions_of(count, total, most, lean, full):
    portions = [(1 << 20) // math.isqrt(standing ** lean) + 1 for standing in range(1, count + 1)]
    largest = most if full else min(most, max(-(-total // count), total * portions[0] // sum(portions)))
    least = 1 if total - largest >= count - 1 else 0
    holding, surplus = [largest] + [least] * (count - 1), total - largest - least * (count - 1)
    while surplus > 0:
        movable = [i for i in range(1, count) if holding[i] < largest] or [i for i in range(1, count) if holding[i] < most]
        mass, left = sum([portions[i] for i in movable]), surplus
        for i in movable:
            more = min(most - holding[i], max(1, left * portions[i] // mass), surplus)
            holding[i] = holding[i] + more
            surplus = surplus - more
    return np.array(holding)


def gaussian(key, extent, deviation, reach, split=(), held_as=jnp.bfloat16):
    entries = deviation * jax.random.normal(key, extent, jnp.float32)
    if split:
        entries = entries * shard_levels(key, extent, split, -0.22, 0.18)
    return jnp.clip(entries, -reach, reach).astype(held_as)


def setup_inputs(seed: int = 0) -> dict:
    seeds = jax.random.split(jax.random.key(seed), 9)
    x_tokens = draw_x_tokens(jax.random.fold_in(seeds[8], 71), 0)
    router_weight = draw_router_weight(jax.random.fold_in(seeds[8], 71), 0)
    gate_rest = gaussian(seeds[2], (TOKENS, EXPERTS - WIN), 32.0, 192.0, ((0, 128),), jnp.float32)
    latent_in = gaussian(seeds[3], (TOKENS, L), 1.0, 6.0, ((0, 128),))
    latent_grad = gaussian(seeds[4], (TOKENS, L), 1.0, 6.0, ((0, 128),))
    expert_picks_keys = jax.random.split(jax.random.fold_in(seeds[5], 1), TOKENS // TOK_DEV)
    expert_picks_turns = jax.random.permutation(jax.random.fold_in(seeds[5], 3), TOKENS // TOK_DEV)
    expert_picks = jax.vmap(lambda own, number: routed_block(jax.random.fold_in(seeds[5], 2), own, number, TOK_DEV, EXPERTS, TOP, SLOT_DEPTH, 2))(expert_picks_keys, expert_picks_turns).reshape((TOKENS, TOP))
    expert_in = gaussian(seeds[6], (BLOCKS, L, HB), L ** -0.5, 0.1875, ((0, 32),))
    expert_out = gaussian(seeds[7], (BLOCKS, HB, L), H ** -0.5, 0.125, ((0, 32),))
    return {"x_tokens": x_tokens, "router_weight": router_weight, "gate_rest": gate_rest, "latent_in": latent_in, "latent_grad": latent_grad, "expert_picks": expert_picks, "expert_in": expert_in, "expert_out": expert_out}


def reference(x_tokens, router_weight, gate_rest, latent_in, latent_grad, expert_picks, expert_in, expert_out):
    logits = jnp.dot(x_tokens, router_weight, preferred_element_type=jnp.float32)
    probs = jax.nn.softmax(logits, axis=-1)
    window_ids = jnp.arange(WIN, dtype=jnp.int32)
    chosen = jnp.any(expert_picks[:, :, None] == window_ids[None, None, :], axis=1)
    picked_probs = jnp.where(chosen, probs[:, :WIN], jnp.float32(0.0))
    full_in = jnp.transpose(expert_in.reshape(WIN, 2, L, HB), (0, 2, 1, 3)).reshape(WIN, L, H)
    full_out = expert_out.reshape(WIN, H, L)

    def one_expert(running, item):
        weight_a, weight_b, column = item
        preact = jnp.dot(latent_in, weight_a, preferred_element_type=jnp.float32)
        hidden_grad = jnp.dot(latent_grad, weight_b.T, preferred_element_type=jnp.float32)
        active = jnp.maximum(preact, 0.0)
        gate_column = jnp.sum(active * active * hidden_grad, axis=1)
        coeff = (column[:, None] * 2.0 * active * hidden_grad).astype(jnp.bfloat16)
        running = running + jnp.dot(coeff, weight_a.T, preferred_element_type=jnp.float32)
        return running, gate_column

    initial = jnp.zeros((TOKENS, L), jnp.float32)
    latent_sum, gate_columns = lax.scan(one_expert, initial, (full_in, full_out, picked_probs.T))
    gate_grad = jnp.concatenate([gate_columns.T, gate_rest], axis=1)
    centre = jnp.sum(probs * gate_grad, axis=-1, keepdims=True)
    logit_grad = probs * (gate_grad - centre)
    logit_low = logit_grad.astype(jnp.bfloat16)
    x_grad = jnp.dot(logit_low, router_weight.T, preferred_element_type=jnp.float32).astype(jnp.bfloat16)
    router_weight_grad = jnp.dot(x_tokens.T, logit_low, preferred_element_type=jnp.float32)
    return latent_sum.astype(jnp.bfloat16), x_grad, router_weight_grad
```

```python
import functools

import jax
import jax.numpy as jnp
from jax import lax
from jax.experimental import pallas as pl
from jax.experimental.pallas import tpu as pltpu
from jax.sharding import Mesh
from jax.sharding import PartitionSpec as P

F32 = jnp.float32
BF16 = jnp.bfloat16
NT = (((1,), (1,)), ((), ()))
NN = (((1,), (0,)), ((), ()))
AXES = ("yl", "co", "x", "z", "yh")
PLANE = ("x", "z")
OCTET = ("yl", "co", "yh")
SLOTS = 16


def gate_kernel(t_ref, w_ref, v_ref, o_ref):
    width = w_ref.shape[1]
    rows = t_ref.shape[0]
    tile = 512

    @pl.when(pl.program_id(0) == 0)
    def _():
        o_ref[...] = jnp.zeros_like(o_ref)

    for start in range(0, rows, tile):
        here = slice(start, min(rows, start + tile))
        pre = lax.dot_general(w_ref[...], t_ref[here, :width], NT, preferred_element_type=F32)
        grad = lax.dot_general(v_ref[...], t_ref[here, width:], NT, preferred_element_type=F32)
        active = jnp.maximum(pre, 0.0)
        piece = active * active * grad
        o_ref[:, here] += jnp.sum(piece, axis=0, keepdims=True)


def gate_sums(tokens, w_t, v):
    rows, both = tokens.shape
    hidden, width = w_t.shape
    tile = hidden // 3
    return pl.pallas_call(
        gate_kernel,
        grid=(3,),
        in_specs=[
            pl.BlockSpec((rows, both), lambda i: (0, 0)),
            pl.BlockSpec((tile, width), lambda i: (i, 0)),
            pl.BlockSpec((tile, width), lambda i: (i, 0)),
        ],
        out_specs=pl.BlockSpec((1, rows), lambda i: (0, 0)),
        out_shape=jax.ShapeDtypeStruct((1, rows), F32),
        compiler_params=pltpu.CompilerParams(vmem_limit_bytes=40 << 20),
        cost_estimate=pl.CostEstimate(
            flops=4 * rows * hidden * width, bytes_accessed=4 * hidden * width + 2 * rows * both, transcendentals=0
        ),
    )(tokens, w_t, v)


def slots_of(hits):
    rows = hits.shape[1]
    upper = (jnp.arange(rows)[:, None] <= jnp.arange(rows)[None, :]).astype(BF16)
    rank = jnp.dot(hits.astype(BF16), upper, preferred_element_type=F32)
    return jnp.where(hits, rank - 1.0, -1.0)


def shards(
    x_tokens, router_weight, gate_rest, latent_in, latent_grad, expert_picks, expert_in, expert_out
):
    co = lax.axis_index("co")
    px = lax.axis_index("x")
    pz = lax.axis_index("z")
    yh = lax.axis_index("yh")
    my_expert = px * 4 + pz
    rows = x_tokens.shape[0]
    width = latent_in.shape[1]

    def along(first, step):
        pairs = []
        for c in range(2):
            for i in range(4):
                for j in range(4):
                    in_x = (c == 0) == first
                    to = ((i + step) % 4) * 4 + j if in_x else i * 4 + (j + step) % 4
                    pairs.append((c * 16 + i * 4 + j, c * 16 + to))
        return lambda value: lax.ppermute(value, ("co", "x", "z"), pairs)

    own = jnp.concatenate([latent_in, latent_grad], axis=1)
    half = rows // 2
    up1 = along(True, 1)(own)
    down1 = along(True, -1)(own)
    up2 = along(True, 1)(up1[:half])
    down2 = along(True, -1)(down1[half:])
    line = jnp.concatenate([own, up1, down1, up2, down2], axis=0)
    line_up = along(False, 1)(line)
    line_down = along(False, -1)(line)
    far_up = along(False, 1)(line_up[: 2 * rows])
    far_down = along(False, -1)(line_down[2 * rows :])

    w_t = expert_in[0].T
    v = expert_out[0]
    hidden = v.shape[0]
    cut = hidden // 2
    stacked = jnp.concatenate([w_t, v], axis=1)
    part = lax.dynamic_slice_in_dim(stacked, co * cut, cut, 0)
    got = lax.ppermute(part, ("yl", "yh"), [(2, 1), (1, 2), (3, 0), (0, 3)])
    got_other = lax.ppermute(got, "co", [(0, 1), (1, 0)])
    weights = [(w_t, v)] + [(g[:, :width], g[:, width:]) for g in (got, got_other)]

    logits = jnp.dot(x_tokens, router_weight, preferred_element_type=F32)
    probs = jax.nn.softmax(logits, axis=-1)
    experts = logits.shape[1]
    window = 16
    x_t = x_tokens.T.reshape(4, 16, 2, 32, rows).transpose(0, 2, 1, 3, 4).reshape(8, 512, rows)
    x_cols = lax.all_to_all(x_t, OCTET, 0, 0, tiled=True)
    x_cols = x_cols.transpose(1, 0, 2).reshape(512, 8 * rows)

    groups = [line, line_up, line_down, jnp.concatenate([far_up, far_down], axis=0)]
    gates = []
    for tokens in groups:
        total = gate_sums(tokens, w_t, v)
        for piece_w, piece_v in weights[1:]:
            total = total + gate_sums(tokens, piece_w, piece_v)
        gates.append(total.reshape(4, rows))
    gates = jnp.concatenate(gates, axis=0)

    offsets = jnp.array([0, -1, 1, 2], dtype=jnp.int32)
    first = jnp.tile(offsets, 4)
    second = jnp.repeat(offsets, 4)
    dx = jnp.where(co == 0, first, second)
    dz = jnp.where(co == 0, second, first)
    source = ((px + dx) % 4) * 4 + (pz + dz) % 4
    place = source[None, :] == jnp.arange(16, dtype=jnp.int32)[:, None]

    gates_abs = jnp.dot(place.astype(F32), gates, precision=lax.Precision.HIGHEST)
    gate_back = lax.all_to_all(gates_abs, PLANE, 0, 0, tiled=True)

    picks = lax.dynamic_slice_in_dim(expert_picks.reshape(16, 2, rows, -1), yh, 1, 1)[:, 0]
    hits = jnp.any(picks == my_expert, axis=2)
    slot_abs = slots_of(hits)
    slot_rel = jnp.dot(place.T.astype(BF16), slot_abs.astype(BF16), preferred_element_type=F32)
    slot_ids = jnp.arange(SLOTS, dtype=F32)
    choose = (place[:, None, :, None]) & (slot_rel[None, None] == slot_ids[None, :, None, None])
    choose = choose.reshape(16 * SLOTS, 16 * rows).astype(BF16)
    tokens = jnp.concatenate(groups, axis=0)
    chosen = jnp.dot(choose, tokens, preferred_element_type=F32).astype(BF16)
    terms = jnp.zeros((16 * SLOTS, width), F32)
    for piece_w, piece_v in weights:
        pre = lax.dot_general(chosen[:, :width], piece_w, NT, preferred_element_type=F32)
        grad = lax.dot_general(chosen[:, width:], piece_v, NT, preferred_element_type=F32)
        coeff = (2.0 * jnp.maximum(pre, 0.0) * grad).astype(BF16)
        terms = terms + jnp.dot(coeff, piece_w, preferred_element_type=F32)
    terms = terms.astype(BF16).reshape(16, SLOTS, width)
    back = lax.all_to_all(terms, PLANE, 0, 0, tiled=True).reshape(16 * SLOTS, width)

    gate_window = gate_back.T
    gate_grad = jnp.concatenate([gate_window, gate_rest], axis=1)
    centre = jnp.sum(probs * gate_grad, axis=-1, keepdims=True)
    logit_low = (probs * (gate_grad - centre)).astype(BF16)
    swap = [(0, 1), (1, 0)]
    near = lax.ppermute(logit_low, ("yl", "yh"), [(2, 1), (1, 2), (3, 0), (0, 3)])
    side = lax.ppermute(logit_low, "yl", swap)
    far = lax.ppermute(logit_low, "yh", swap)
    mine = jnp.stack([logit_low, near, side, far])
    theirs = lax.ppermute(mine, "co", swap)
    yl = lax.axis_index("yl")
    me4 = yl * 2 + yh
    origin = jnp.stack([me4, 3 - me4, (1 - yl) * 2 + yh, yl * 2 + 1 - yh])
    rows8 = jnp.concatenate([mine, theirs], axis=0)
    core8 = jnp.concatenate([jnp.full((4,), co), jnp.full((4,), 1 - co)])
    origin8 = jnp.concatenate([origin, origin])
    index8 = (origin8 // 2) * 4 + core8 * 2 + origin8 % 2
    x_blocks = x_cols.reshape(512, 8, rows)
    partial = jnp.zeros((512, experts), F32)
    for k in range(8):
        block = lax.dynamic_slice_in_dim(x_blocks, index8[k], 1, 1)[:, 0]
        partial = partial + jnp.dot(block, rows8[k], preferred_element_type=F32)
    spread = lax.all_to_all(partial.reshape(16, 32, experts), PLANE, 0, 0, tiled=True)
    router_weight_grad = jnp.sum(spread, axis=0)

    x_grad = lax.dot_general(logit_low, router_weight, NT, preferred_element_type=F32).astype(BF16)

    lane = my_expert * 2 + yh
    own_picks = lax.dynamic_slice_in_dim(expert_picks, lane * rows, rows, 0)
    own_hits = jnp.any(own_picks[None] == jnp.arange(16, dtype=jnp.int32)[:, None, None], axis=2)
    own_slots = slots_of(own_hits)
    spot = own_slots[:, None, :] == slot_ids[None, :, None]
    scale = jnp.where(spot, probs[:, :window].T[:, None, :], 0.0).reshape(16 * SLOTS, rows)
    high = lax.reduce_precision(scale, 8, 7)
    low = scale - high
    tn = (((0,), (0,)), ((), ()))
    latent_sum = lax.dot_general(high.astype(BF16), back, tn, preferred_element_type=F32)
    latent_sum = latent_sum + lax.dot_general(low.astype(BF16), back, tn, preferred_element_type=F32)
    return (latent_sum.astype(BF16), x_grad, router_weight_grad)


def solution(mesh):
    fine = Mesh(mesh.devices.reshape(2, 2, 4, 4, 2), AXES)
    every = P(AXES, None)
    blocks = P(("x", "z", "yh"), None, None)
    placed = (every, P(), every, every, every, P(("yl", "co"), None), blocks, blocks)
    return jax.shard_map(
        shards, mesh=fine, in_specs=placed, out_specs=(every, every, every), check_vma=False
    )
```

```python
import jax
import jax.numpy as jnp
from jax import lax
from jax.experimental import pallas as pl
from jax.experimental.pallas import tpu as pltpu
from jax.sharding import Mesh
from jax.sharding import PartitionSpec as P

F32 = jnp.float32
BF16 = jnp.bfloat16
NT = (((1,), (1,)), ((), ()))
TN = (((0,), (0,)), ((), ()))
AXES = ("yl", "co", "x", "z", "yh")
PLANE = ("x", "z")
OCTET = ("yl", "co", "yh")
SLOTS = 16
FIRST_CUT = 512


ANY = pl.BlockSpec(memory_space=pl.ANY)
VMEM = pl.BlockSpec(memory_space=pltpu.VMEM)


def join(*parts):
    sizes = [part.shape[0] for part in parts]
    width = parts[0].shape[1]

    def kernel(*refs):
        start = 0
        for ref, size in zip(refs[:-1], sizes):
            refs[-1][start : start + size, :] = ref[...]
            start += size

    return pl.pallas_call(
        kernel,
        in_specs=[VMEM] * len(parts),
        out_specs=VMEM,
        out_shape=jax.ShapeDtypeStruct((sum(sizes), width), parts[0].dtype),
        cost_estimate=pl.CostEstimate(
            flops=0, bytes_accessed=4 * sum(sizes) * width, transcendentals=0
        ),
    )(*parts)


def side_by_side(left, right):
    rows, width = left.shape

    def kernel(a, b, out):
        out[:, :width] = a[...]
        out[:, width:] = b[...]

    return pl.pallas_call(
        kernel,
        in_specs=[VMEM] * 2,
        out_specs=VMEM,
        out_shape=jax.ShapeDtypeStruct((rows, width + right.shape[1]), left.dtype),
    )(left, right)


def fetch(pairs, sems, first):
    copies = [
        pltpu.make_async_copy(src, dst, sems.at[first + k]) for k, (src, dst) in enumerate(pairs)
    ]
    for copy in copies:
        copy.start()
    return copies


def gate_sums(groups, pieces):
    parts = [part for group in groups for part in group]
    flat = [array for piece in pieces for array in piece]
    both = parts[0].shape[1]
    width = both // 2
    span = sum(part.shape[0] for part in groups[0])
    count = len(groups)
    shapes = []
    for piece in pieces:
        if isinstance(piece, tuple):
            shapes += [piece[0].shape, piece[1].shape]
        else:
            shapes += [(sum(array.shape[0] for array in piece), both)]
    hidden = sum(p[0].shape[0] if isinstance(p, tuple) else sum(a.shape[0] for a in p) for p in pieces)

    def kernel(*refs):
        n_parts, n_flat = len(parts), len(flat)
        part_refs = refs[:n_parts]
        flat_refs = list(refs[n_parts : n_parts + n_flat])
        out = refs[n_parts + n_flat]
        held = refs[n_parts + n_flat + 1]
        weights = list(refs[n_parts + n_flat + 2 : -1])
        sems = refs[-1]
        token_pairs = []
        at = 0
        for g, group in enumerate(groups):
            start = 0
            for part in group:
                token_pairs.append((part_refs[at], held.at[g, pl.ds(start, part.shape[0])]))
                start += part.shape[0]
                at += 1
        weight_pairs = []
        views = []
        k = 0
        for piece in pieces:
            if isinstance(piece, tuple):
                weight_pairs += list(zip(flat_refs[:2], weights[k : k + 2]))
                flat_refs = flat_refs[2:]
                views.append((weights[k], weights[k + 1], 0))
                k += 2
            else:
                start = 0
                for array in piece:
                    weight_pairs.append((flat_refs.pop(0), weights[k].at[pl.ds(start, array.shape[0])]))
                    start += array.shape[0]
                views.append((weights[k], weights[k], width))
                k += 1
        near = len(groups[0])
        first_copies = fetch(token_pairs[:near], sems, 0)
        weight_copies = fetch(weight_pairs, sems, n_parts)
        rest = fetch(token_pairs[near:], sems, near)
        for copy in first_copies + weight_copies:
            copy.wait()

        def one(g):
            total = jnp.zeros((1, span), F32)
            for w, v, shift in views:
                size = w.shape[0]
                steps = max(1, size // 448)
                tile = size // steps
                for i in range(steps):
                    here = slice(i * tile, (i + 1) * tile)
                    pre = lax.dot_general(
                        w[here, :width], held[g, :, :width], NT, preferred_element_type=F32
                    )
                    grad = lax.dot_general(
                        v[here, shift : shift + width], held[g, :, width:], NT, preferred_element_type=F32
                    )
                    active = jnp.maximum(pre, 0.0)
                    total = total + jnp.sum(active * active * grad, axis=0, keepdims=True)
            out[pl.ds(g, 1), :] = total

        @pl.loop(0, count)
        def _(g):
            if count > 1:

                @pl.when(g == 1)
                def _():
                    for copy in rest:
                        copy.wait()

            one(g)

    scratch = [pltpu.VMEM((count, span, both), BF16)]
    scratch += [pltpu.VMEM(shape, BF16) for shape in shapes]
    scratch += [pltpu.SemaphoreType.DMA((len(parts) + len(flat),))]
    return pl.pallas_call(
        kernel,
        in_specs=[ANY] * (len(parts) + len(flat)),
        out_specs=VMEM,
        out_shape=jax.ShapeDtypeStruct((count, span), F32),
        scratch_shapes=scratch,
        compiler_params=pltpu.CompilerParams(vmem_limit_bytes=40 << 20),
        cost_estimate=pl.CostEstimate(
            flops=4 * count * span * hidden * width,
            bytes_accessed=4 * hidden * width + 2 * count * span * both,
            transcendentals=0,
        ),
    )(*parts, *flat)


def select_rows(choose, copies, held, rows):
    start = 0
    for copy, ref in zip(copies, held):
        copy.wait()
        size = ref.shape[0]
        rows = rows + jnp.dot(choose[:, start : start + size], ref[...], preferred_element_type=F32)
        start += size
    return rows


def pick_rows(choose, parts):
    count = choose.shape[0]
    both = parts[0].shape[1]
    n = len(parts)

    def kernel(*refs):
        copies = fetch(list(zip(refs[1 : 1 + n], refs[2 + n : 2 + 2 * n])), refs[-1], 0)
        rows = select_rows(refs[0], copies, refs[2 + n : 2 + 2 * n], jnp.zeros((count, both), F32))
        refs[1 + n][...] = rows.astype(BF16)

    return pl.pallas_call(
        kernel,
        in_specs=[VMEM] + [ANY] * n,
        out_specs=VMEM,
        out_shape=jax.ShapeDtypeStruct((count, both), BF16),
        scratch_shapes=[pltpu.VMEM(part.shape, BF16) for part in parts]
        + [pltpu.SemaphoreType.DMA((n,))],
        compiler_params=pltpu.CompilerParams(vmem_limit_bytes=40 << 20),
        cost_estimate=pl.CostEstimate(
            flops=2 * choose.size * both, bytes_accessed=2 * choose.size, transcendentals=0
        ),
    )(choose, *parts)


def picked_terms(chosen, choose, parts, pieces):
    flat = [array for piece in pieces for array in (piece if isinstance(piece, tuple) else (piece,))]
    count, both = chosen.shape
    width = both // 2
    hidden = sum((p[0] if isinstance(p, tuple) else p).shape[0] for p in pieces)
    n, m = len(parts), len(flat)

    def kernel(*refs):
        part_refs, flat_refs = refs[2 : 2 + n], refs[2 + n : 2 + n + m]
        out = refs[2 + n + m]
        held, weights = refs[3 + n + m : 3 + 2 * n + m], refs[3 + 2 * n + m : 3 + 2 * n + 2 * m]
        sems = refs[-1]
        token_copies = fetch(list(zip(part_refs, held)), sems, 0)
        weight_copies = fetch(list(zip(flat_refs, weights)), sems, n)
        rows = select_rows(refs[1], token_copies, held, refs[0][...].astype(F32)).astype(BF16)
        terms = jnp.zeros((count, width), F32)
        k = 0
        for piece in pieces:
            if isinstance(piece, tuple):
                weight_copies[k].wait()
                weight_copies[k + 1].wait()
                w, v, k = weights[k][...], weights[k + 1][...], k + 2
            else:
                weight_copies[k].wait()
                w, v, k = weights[k][:, :width], weights[k][:, width:], k + 1
            pre = lax.dot_general(rows[:, :width], w, NT, preferred_element_type=F32)
            grad = lax.dot_general(rows[:, width:], v, NT, preferred_element_type=F32)
            coeff = (2.0 * jnp.maximum(pre, 0.0) * grad).astype(BF16)
            terms = terms + jnp.dot(coeff, w, preferred_element_type=F32)
        out[...] = terms.astype(BF16)

    return pl.pallas_call(
        kernel,
        in_specs=[VMEM] * 2 + [ANY] * (n + m),
        out_specs=VMEM,
        out_shape=jax.ShapeDtypeStruct((count, width), BF16),
        scratch_shapes=[pltpu.VMEM(array.shape, BF16) for array in list(parts) + flat]
        + [pltpu.SemaphoreType.DMA((n + m,))],
        compiler_params=pltpu.CompilerParams(vmem_limit_bytes=48 << 20),
        cost_estimate=pl.CostEstimate(
            flops=6 * count * hidden * width, bytes_accessed=4 * hidden * width, transcendentals=0
        ),
    )(chosen, choose, *parts, *flat)


def slots_of(hits):
    rows = hits.shape[1]
    upper = (jnp.arange(rows)[:, None] <= jnp.arange(rows)[None, :]).astype(BF16)
    rank = jnp.dot(hits.astype(BF16), upper, preferred_element_type=F32)
    return jnp.where(hits, rank - 1.0, -1.0)


def after(value, *others):
    return lax.optimization_barrier((value, *others))[0]


def shards(
    x_tokens, router_weight, gate_rest, latent_in, latent_grad, expert_picks, expert_in, expert_out
):
    co = lax.axis_index("co")
    px = lax.axis_index("x")
    pz = lax.axis_index("z")
    yh = lax.axis_index("yh")
    yl = lax.axis_index("yl")
    my_expert = px * 4 + pz
    rows = x_tokens.shape[0]
    width = latent_in.shape[1]
    half = rows // 2
    swap = [(0, 1), (1, 0)]
    cross = [(2, 1), (1, 2), (3, 0), (0, 3)]

    def along(first, step, value):
        pairs = []
        for c in range(2):
            for i in range(4):
                for j in range(4):
                    in_x = (c == 0) == first
                    to = ((i + step) % 4) * 4 + j if in_x else i * 4 + (j + step) % 4
                    pairs.append((c * 16 + i * 4 + j, c * 16 + to))
        return lax.ppermute(value, ("co", "x", "z"), pairs)

    own = side_by_side(latent_in, latent_grad)
    up1 = along(True, 1, own)
    down1 = along(True, -1, own)

    w_t = expert_in[0].T
    v = expert_out[0]
    hidden = v.shape[0]
    cut = hidden // 2
    part = jnp.concatenate(
        [
            lax.dynamic_slice_in_dim(w_t, co * cut, cut, 0),
            lax.dynamic_slice_in_dim(v, co * cut, cut, 0),
        ],
        axis=1,
    )
    part0, part1 = part[:FIRST_CUT], part[FIRST_CUT:]
    got0 = lax.ppermute(part0, ("yl", "yh"), cross)
    got1 = lax.ppermute(part1, ("yl", "yh"), cross)
    other0 = lax.ppermute(got0, "co", swap)
    other1 = lax.ppermute(got1, "co", swap)

    up2 = along(True, 1, up1[:half])
    down2 = along(True, -1, down1[half:])
    line_a = join(own, up1)
    line_b = join(down1, up2, down2)
    up_a = along(False, 1, line_a)
    down_a = along(False, -1, line_a)
    up_b = along(False, 1, line_b)
    down_b = along(False, -1, line_b)
    far_up = along(False, 1, up_a)
    far_down = along(False, -1, down_b)

    logits = jnp.dot(after(x_tokens, up2), router_weight, preferred_element_type=F32)
    probs = jax.nn.softmax(logits, axis=-1)
    experts = logits.shape[1]
    window = 16
    x_t = after(x_tokens, up2).T.reshape(4, 16, 2, 32, rows).transpose(0, 2, 1, 3, 4)
    x_t = x_t.reshape(8, 512, rows)
    x_cols = lax.all_to_all(x_t, OCTET, 0, 0, tiled=True)

    places = [(yl, yh), (1 - yl, 1 - yh), (1 - yl, yh), (yl, 1 - yh)]
    index8 = [a * 4 + c * 2 + b for c in (co, 1 - co) for a, b in places]
    picked = [lax.dynamic_slice_in_dim(x_cols, index8[k], 1, 0)[0] for k in range(8)]
    x_mine = jnp.concatenate(picked[:4], axis=1)
    x_theirs = jnp.concatenate(picked[4:], axis=1)
    offsets = jnp.array([0, -1, 1, 2], dtype=jnp.int32)
    first = jnp.tile(offsets, 4)
    second = jnp.repeat(offsets, 4)
    dx = jnp.where(co == 0, first, second)
    dz = jnp.where(co == 0, second, first)
    source = ((px + dx) % 4) * 4 + (pz + dz) % 4
    place = source[None, :] == jnp.arange(16, dtype=jnp.int32)[:, None]

    picks = lax.dynamic_slice_in_dim(
        after(expert_picks, up2).reshape(16, 2, rows, -1), yh, 1, 1
    )[:, 0]
    hits = jnp.any(picks == my_expert, axis=2)
    slot_abs = slots_of(hits)
    slot_rel = jnp.dot(place.T.astype(BF16), slot_abs.astype(BF16), preferred_element_type=F32)
    slot_ids = jnp.arange(SLOTS, dtype=F32)
    choose = (place[:, None, :, None]) & (slot_rel[None, None] == slot_ids[None, :, None, None])
    choose = choose.reshape(16 * SLOTS, 16 * rows).astype(BF16)
    lane = my_expert * 2 + yh
    own_picks = lax.dynamic_slice_in_dim(after(expert_picks, up2), lane * rows, rows, 0)
    own_hits = jnp.any(own_picks[None] == jnp.arange(16, dtype=jnp.int32)[:, None, None], axis=2)
    own_slots = slots_of(own_hits)
    spot = own_slots[:, None, :] == slot_ids[None, :, None]
    scale = jnp.where(spot, probs[:, :window].T[:, None, :], 0.0).reshape(16 * SLOTS, rows)
    high = lax.reduce_precision(scale, 8, 7)
    low = scale - high
    mine = (w_t, v)
    near_groups = [[line_a, line_b], [up_a, up_b], [down_a, down_b]]
    far_group = [[far_up, far_down]]
    near_parts = [part for group in near_groups for part in group]
    near_rows = 12 * rows
    g_line = gate_sums(near_groups[:1], [mine])
    g_sides = gate_sums(near_groups[1:], [mine])
    chosen_near = pick_rows(choose[:, :near_rows], near_parts)
    g_near = gate_sums(near_groups, [[got0, other0]])
    g_far = gate_sums(far_group, [mine, [got0, other0]])
    g_last = gate_sums(near_groups + far_group, [[got1, other1]])
    gates = jnp.concatenate([jnp.concatenate([g_line, g_sides], axis=0) + g_near, g_far], axis=0)
    gates = (gates + g_last).reshape(16, rows)

    gates_abs = jnp.dot(place.astype(F32), gates, precision=lax.Precision.HIGHEST)
    gate_back = lax.all_to_all(gates_abs, PLANE, 0, 0, tiled=True)

    lane = my_expert * 2 + yh
    own_picks = lax.dynamic_slice_in_dim(after(expert_picks, up2), lane * rows, rows, 0)
    own_hits = jnp.any(own_picks[None] == jnp.arange(16, dtype=jnp.int32)[:, None, None], axis=2)
    own_slots = slots_of(own_hits)
    spot = own_slots[:, None, :] == slot_ids[None, :, None]
    scale = jnp.where(spot, probs[:, :window].T[:, None, :], 0.0).reshape(16 * SLOTS, rows)
    high = lax.reduce_precision(scale, 8, 7)
    low = scale - high
    mine = (w_t, v)
    near_groups = [[line_a, line_b], [up_a, up_b], [down_a, down_b]]
    far_group = [[far_up, far_down]]
    near_parts = [part for group in near_groups for part in group]
    near_rows = 12 * rows
    g_line = gate_sums(near_groups[:1], [mine])
    g_sides = gate_sums(near_groups[1:], [mine])
    chosen_near = pick_rows(choose[:, :near_rows], near_parts)
    g_near = gate_sums(near_groups, [[got0, other0]])
    g_far = gate_sums(far_group, [mine, [got0, other0]])
    g_last = gate_sums(near_groups + far_group, [[got1, other1]])
    gates = jnp.concatenate([jnp.concatenate([g_line, g_sides], axis=0) + g_near, g_far], axis=0)
    gates = (gates + g_last).reshape(16, rows)

    gates_abs = jnp.dot(place.astype(F32), gates, precision=lax.Precision.HIGHEST)
    gate_back = lax.all_to_all(gates_abs, PLANE, 0, 0, tiled=True)

    terms = picked_terms(
        chosen_near, choose[:, near_rows:], [far_up, far_down],
        [mine, got0, other0, got1, other1],
    )
    back = lax.all_to_all(terms.reshape(16, SLOTS, width), PLANE, 0, 0, tiled=True)
    back = back.reshape(16 * SLOTS, width)

    gate_grad = jnp.concatenate([gate_back.T, gate_rest], axis=1)
    centre = jnp.sum(probs * gate_grad, axis=-1, keepdims=True)
    logit_low = (probs * (gate_grad - centre)).astype(BF16)
    near = lax.ppermute(logit_low, ("yl", "yh"), cross)
    side = lax.ppermute(logit_low, "yl", swap)
    far = lax.ppermute(logit_low, "yh", swap)
    mine4 = jnp.concatenate([logit_low, near, side, far], axis=0)
    theirs4 = lax.ppermute(mine4, "co", swap)
    partial = jnp.dot(x_mine, mine4, preferred_element_type=F32)
    partial = partial + jnp.dot(x_theirs, theirs4, preferred_element_type=F32)
    spread = lax.all_to_all(partial.reshape(16, 32, experts), PLANE, 0, 0, tiled=True)
    router_weight_grad = jnp.sum(spread, axis=0)

    x_grad = lax.dot_general(
        after(logit_low, near), router_weight, NT, preferred_element_type=F32
    ).astype(BF16)

    latent_sum = lax.dot_general(high.astype(BF16), back, TN, preferred_element_type=F32)
    latent_sum = latent_sum + lax.dot_general(low.astype(BF16), back, TN, preferred_element_type=F32)
    latent_sum = latent_sum.astype(BF16)
    return (latent_sum, x_grad, router_weight_grad)


def solution(mesh):
    fine = Mesh(mesh.devices.reshape(2, 2, 4, 4, 2), AXES)
    every = P(AXES, None)
    blocks = P(("x", "z", "yh"), None, None)
    placed = (every, P(), every, every, every, P(("yl", "co"), None), blocks, blocks)

    return jax.shard_map(
        shards, mesh=fine, in_specs=placed, out_specs=(every, every, every), check_vma=False
    )
```
